32 devices in a mesh: groups: 2 (over y), row: 4 (over x, core), col: 4 (over z).
Axes of the slice: x: 2, y: 2, z: 4, core: 2. Of those that a mesh axis runs over, the one named last changes fastest.
Arguments:
- inputs: bfloat16 [1536, 4096], P(('groups', 'col'), 'row'), parts along dimension 0, may hold values from -6 to 6
- cotangent: bfloat16 [1536, 4096], P(('groups', 'col'), 'row'), parts along dimension 0, may hold values from -6 to 6
- preactivation: bfloat16 [1536, 8192], P(('groups', 'row'), 'col'), parts along dimension 0, may hold values from -8 to 8
- up_weight: bfloat16 [4096, 8192], P('row', 'col'), may hold values from -0.09375 to 0.09375
- down_weight: bfloat16 [8192, 4096], P('col', 'row'), may hold values from -0.0625 to 0.0625
Outputs:
- grad_input: bfloat16 [1536, 4096], P(('groups', 'col'), 'row'), parts along dimension 0
- grad_up: float32 [8192, 8192], P(('groups', 'row'), 'col'), parts along dimension 0
- grad_down: float32 [16384, 4096], P(('groups', 'col'), 'row'), parts along dimension 0
The draws below stay inside these ranges and needn't reach their ends.
There are 2 independent parts, one for each index of `groups`. The reference program is written for one: setup_inputs(seed, part) draws one part's arguments, and reference() takes and returns one part's arrays. A program takes and returns all parts, laid end to end along the dimension named above; an argument that names none is the same for every part. Nothing has to cross between parts.
All inputs are finite; a program needn't handle non-finite values.
Results may differ from the reference program's by a relative error of at most 0.0049.
Values may be sent and summed in bfloat16 or wider, within the bound.
A program may use at most 128 MiB of HBM per device.

```python
import jax
import jax.numpy as jnp

D = 4096
H = 8192
TOKENS = 768


def block_scale(key, extent, cuts, smallest, top_value):
    level, own = 1.0, jax.random.fold_in(key, 6)
    for axis_at, blocks in cuts:
        draws = jnp.exp(jax.random.uniform(jax.random.fold_in(own, axis_at), (blocks,), jnp.float32, smallest / len(cuts), top_value / len(cuts)))
        level = level * jnp.repeat(draws, extent[axis_at] // blocks).reshape([-1 if axis == axis_at else 1 for axis in range(len(extent))])
    return level


def scatter_about(own_key, shape, deviation, reach, pieces=(), dtype=jnp.bfloat16):
    result = jax.random.normal(own_key, shape, jnp.float32) * deviation
    if len(pieces) > 0:
        result = block_scale(own_key, shape, pieces, -0.22, 0.18) * result
    return jnp.clip(result, min=-reach, max=reach).astype(dtype)


def setup_inputs(seed: int = 0, part: int = 0) -> dict:
    key_list = jax.random.split(jax.random.key(seed), 6)
    part_keys = jax.random.split(jax.random.fold_in(key_list[5], part), 6)
    return {
        "inputs": scatter_about(part_keys[0], (TOKENS, D), 1.0, 6.0, ((0, 4), (1, 4))),
        "cotangent": scatter_about(part_keys[1], (TOKENS, D), 1.0, 6.0, ((0, 4), (1, 4))),
        "preactivation": scatter_about(part_keys[2], (TOKENS, H), 1.5, 8.0, ((0, 4), (1, 4))),
        "up_weight": scatter_about(key_list[3], (D, H), D ** -0.5, 0.09375, ((0, 4), (1, 4))),
        "down_weight": scatter_about(key_list[4], (H, D), H ** -0.5, 0.0625, ((0, 4), (1, 4))),
    }


def gelu_pair(values):
    v = values.astype(jnp.float32)
    tanh_arg = 0.7978845608 * (v + 0.044715 * v * v * v)
    tanh_val = jnp.tanh(tanh_arg)
    gelu_value = 0.5 * v * (1.0 + tanh_val)
    gelu_slope = 0.5 * (1.0 + tanh_val) + 0.5 * v * (1.0 - tanh_val * tanh_val) * 0.7978845608 * (1.0 + 3.0 * 0.044715 * v * v)
    return gelu_value, gelu_slope


def reference(inputs, cotangent, preactivation, up_weight, down_weight):
    hidden_grad = jnp.dot(cotangent, down_weight.T, preferred_element_type=jnp.float32)
    gelu_value, gelu_slope = gelu_pair(preactivation)
    activation = gelu_value.astype(jnp.bfloat16)
    pre_grad = (hidden_grad * gelu_slope).astype(jnp.bfloat16)
    grad_input = jnp.dot(pre_grad, up_weight.T, preferred_element_type=jnp.float32).astype(jnp.bfloat16)
    token_scale = 1.0 / (TOKENS ** 0.5)
    grad_up = jnp.dot(inputs.T, pre_grad, preferred_element_type=jnp.float32) * token_scale
    grad_down = jnp.dot(activation.T, cotangent, preferred_element_type=jnp.float32) * token_scale
    return grad_input, grad_up, grad_down
```

```python
import functools
import math

import jax
import jax.numpy as jnp
from jax import lax
from jax.experimental import pallas as pl
from jax.experimental.pallas import tpu as pltpu
from jax.sharding import PartitionSpec as P

F32, BF16 = jnp.float32, jnp.bfloat16
LAST = (((1,), (1,)), ((), ()))
FIRST = (((0,), (0,)), ((), ()))


def tanh_of(v):
    return jnp.tanh(0.7978845608 * (v + 0.044715 * v * v * v))


def gelu_value(values):
    v = values.astype(F32)
    return 0.5 * v * (1.0 + tanh_of(v))


def gelu_pair(values):
    v = values.astype(F32)
    t = tanh_of(v)
    slope = 0.5 * (1.0 + t) + 0.5 * v * (1.0 - t * t) * 0.7978845608 * (1.0 + 3.0 * 0.044715 * v * v)
    return 0.5 * v * (1.0 + t), slope


def remote(src, dst, send, recv, where):
    return pltpu.make_async_remote_copy(
        src_ref=src, dst_ref=dst, send_sem=send, recv_sem=recv, device_id=where,
        device_id_type=pl.DeviceIdType.MESH,
    )


def pick(table, c):
    value = table[0]
    for at, other in enumerate(table):
        if at > 0:
            value = jnp.where(c == at, other, value)
    return value


def visit_order(nc):
    orders = []
    for c in range(nc):
        far = [(j, c, j) if j > c else (nc - 1 - j, nc - 1 - c, j) for j in range(nc) if j != c]
        orders.append([j for _, _, j in sorted(far)])
    return orders


def block_at(c, t, nc):
    near = jnp.minimum(c, nc - 1 - c)
    step = -((t + 1) // 2) if t % 2 else t // 2
    return jnp.where(t <= 2 * near, c + step, jnp.where(2 * c < nc - 1, t, nc - 1 - t))


def kernel(
    nr, nc,
    x_ref, cot_ref, pre_ref, up_ref, down_ref,
    *rest,
):
    gi_ref, x_out, pg_out, gd_out = rest[:4]
    (
    x_all, cot_all, pre_all, act_all, pg_all, up, down, part, h1_out, h1_in, h2_out, h2_in,
    gi_own, gi_acc, gi_out, gi_in, gd_buf,
    loc, cot_s, cot_r, x_s, x_r, pre_s, pre_on, pre_r, h1_s, h1_r, h2_s, h2_r, pg_s, pg_r, gi_s, gi_r,
    x_o, pg_o, gd_o,
    ) = rest[4:]
    r, c = lax.axis_index("row"), lax.axis_index("col")
    nx = nr // 2
    x, k = r // 2, r % 2
    mate_row = 2 * x + (1 - k)
    mate = {"row": mate_row}
    tb, dr = x_ref.shape
    ts, hc = pg_all.shape[1:]
    nq, dq = gi_out.shape[1], gi_out.shape[3]
    hb, eb, gb = min(512, hc), min(256, hc), gd_buf.shape[1]
    peers = [(x + d) % nx for d in range(1, nx)]
    token_scale = 1.0 / math.sqrt(tb * nc)
    end = (c == 0) | (c == nc - 1)
    ends = []

    barrier = pltpu.get_barrier_semaphore()
    for d in range(1, nr):
        pl.semaphore_signal(barrier, inc=1, device_id={"row": (r + d) % nr}, device_id_type=pl.DeviceIdType.MESH)
    for d in range(1, nc):
        pl.semaphore_signal(barrier, inc=1, device_id={"col": (c + d) % nc}, device_id_type=pl.DeviceIdType.MESH)
    local = [
        pltpu.make_async_copy(cot_ref, cot_all.at[c], loc.at[0]),
        pltpu.make_async_copy(down_ref, down, loc.at[1]),
        pltpu.make_async_copy(pre_ref, pre_all.at[pl.ds(r * nc, nc)], loc.at[2]),
        pltpu.make_async_copy(up_ref, up, loc.at[3]),
        pltpu.make_async_copy(x_ref, x_all.at[c], loc.at[4]),
    ]
    for copy in local:
        copy.start()
    pl.semaphore_wait(barrier, nr + nc - 2)

    def started(copy):
        copy.start()
        ends.append(copy)

    def line(all_ref, send, recv, direction, j, source):
        return remote(source, all_ref.at[j], send.at[direction, j], recv.at[j],
                      {"col": c + 1 if direction == 0 else c - 1})

    def pass_on(all_ref, send, recv, own_ref, t):
        for direction, j in ((0, c - t), (1, c + t)):
            there = (j >= 0) & (j < nc)
            onward = (c + 1 < nc) if direction == 0 else (c >= 1)
            jj = jnp.clip(j, 0, nc - 1)
            if t > 0:
                @pl.when(there)
                def _():
                    line(all_ref, send, recv, direction, jj, all_ref.at[jj]).wait_recv()

            @pl.when(there & onward)
            def _():
                src = own_ref if t == 0 else all_ref.at[jj]
                line(all_ref, send, recv, direction, jj, src).start()

    def finish_line(all_ref, send, recv):
        for t in range(nc):
            for direction, j in ((0, c - t), (1, c + t)):
                onward = (c + 1 < nc) if direction == 0 else (c >= 1)
                jj = jnp.clip(j, 0, nc - 1)

                @pl.when((j >= 0) & (j < nc) & onward)
                def _():
                    line(all_ref, send, recv, direction, jj, all_ref.at[jj]).wait_send()

    def pre_send(i, n):
        unit = r * nc + i
        user = unit % nr
        if n == nx - 1:
            target, first = mate_row, True
        else:
            first = user // 2 == peers[n]
            target = jnp.where(first, user, 2 * peers[n] + k)
        return remote(pre_ref.at[i], pre_all.at[unit], pre_s.at[i, n], pre_r.at[unit], {"row": target}), first

    def pre_unit(unit):
        source, user = unit // nc, unit % nr
        away = source // 2 != x
        straight = jnp.where(user // 2 == x, user == r, source % 2 == k)
        return away, away & straight, user == r

    def pre_relay(unit):
        return remote(pre_all.at[unit], pre_all.at[unit], pre_on.at[unit], pre_r.at[unit], mate)

    def pre_arrival(unit):
        pre_relay(unit).wait_recv()

    pass_on(cot_all, cot_s, cot_r, cot_ref, 0)
    for early in (True, False):
        for i in range(nc):
            for n in range(nx - 1) if early else (nx - 1,):
                copy, first = pre_send(i, n)
                if early:
                    pl.when(first)(copy.start)
                else:
                    copy.start()

    def pre_rest():
        for i in range(nc):
            for n in range(nx - 1):
                copy, first = pre_send(i, n)
                pl.when(jnp.logical_not(first))(copy.start)

    def pre_spread():
        def body(unit, _):
            away, straight, mine = pre_unit(unit)

            @pl.when(straight & jnp.logical_not(mine))
            def _():
                pre_arrival(unit)

            @pl.when(straight)
            def _():
                pre_relay(unit).start()
            return 0

        lax.fori_loop(0, nc * nr, body, 0)

    def activate_unit(unit):
        def body(i, _):
            at = pl.ds(pl.multiple_of(i * eb, eb), eb)
            act_all[unit, :, at] = gelu_value(pre_all[unit, :, at]).astype(BF16)
            return 0

        lax.fori_loop(0, hc // eb, body, 0)

    def activate_row(row, wait):
        def body(i, _):
            unit = row * nc + i
            if wait:
                pre_arrival(unit)
            activate_unit(unit)
            return 0

        lax.fori_loop(0, nc, body, 0)

    def activate_rest():
        def body(unit, _):
            away, straight, mine = pre_unit(unit)

            @pl.when(away & jnp.logical_not(straight))
            def _():
                pre_arrival(unit)

            @pl.when(away & jnp.logical_not(mine))
            def _():
                activate_unit(unit)
            return 0

        lax.fori_loop(0, nc * nr, body, 0)

    def s0(t):
        j = block_at(c, t, nc)
        if t == 0:
            local[0].wait()
            local[1].wait()
        block = cot_all[j]

        def body(i, _):
            at = pl.ds(pl.multiple_of(i * hb, hb), hb)
            got = lax.dot_general(block, down[at, :], LAST, preferred_element_type=F32)
            for s in range(nr):
                part[t, s, :, at] = got[s * ts : (s + 1) * ts]
            return 0

        lax.fori_loop(0, hc // hb, body, 0)
        for p in range(nx):
            h1_out[t, p] = part[t, 2 * p + (1 - k)].astype(BF16)
        started(remote(h1_out.at[t], h1_in.at[t], h1_s.at[t], h1_r.at[t], mate))

    def s1(t):
        remote(h1_out.at[t], h1_in.at[t], h1_s.at[t], h1_r.at[t], mate).wait_recv()
        for i, p in enumerate(peers):
            h2_out[t, i] = (part[t, 2 * p + k] + h1_in[t, p].astype(F32)).astype(BF16)
            started(remote(h2_out.at[t, i], h2_in.at[t, i], h2_s.at[t, i], h2_r.at[t, i],
                           {"row": 2 * p + k}))

    def pg_copy(t, index, source_row, target_row):
        unit = pg_all.at[block_at(c, t, nc) * nr + source_row]
        return remote(unit, unit, pg_s.at[t, index], pg_r.at[t, source_row], {"row": target_row})

    def s2(t):
        for i, p in enumerate(peers):
            remote(h2_out.at[t, i], h2_in.at[t, i], h2_s.at[t, i], h2_r.at[t, i],
                   {"row": 2 * p + k}).wait_recv()
        j = block_at(c, t, nc)
        unit = j * nr + r

        @pl.when((unit // nc) // 2 != x)
        def _():
            pre_arrival(unit)

        def body(i, _):
            at = pl.ds(pl.multiple_of(i * eb, eb), eb)
            total = part[t, 2 * x + k, :, at] + h1_in[t, x, :, at].astype(F32)
            for i in range(nx - 1):
                total += h2_in[t, i, :, at].astype(F32)
            value, slope = gelu_pair(pre_all[unit, :, at])
            act_all[unit, :, at] = value.astype(BF16)
            pg_all[unit, :, at] = (total * slope).astype(BF16)
            return 0

        lax.fori_loop(0, hc // eb, body, 0)
        for i, p in enumerate(peers):
            started(pg_copy(t, 1 + i, r, 2 * p + k))
        started(pg_copy(t, 0, r, mate_row))

    def s3(t):
        for i, p in enumerate(peers):
            pg_copy(t, 0, 2 * p + k, mate_row).wait_recv()
            started(pg_copy(t, nx + i, 2 * p + k, mate_row))

    outs = []

    def put_out(copy):
        copy.start()
        outs.append(copy)

    def pg_ready(t):
        for p in range(nx):
            pg_copy(t, 0, 2 * p + (1 - k), mate_row).wait_recv()
        units = pl.ds(block_at(c, t, nc) * nr, nr)
        put_out(pltpu.make_async_copy(pg_all.at[units], pg_out.at[units], pg_o.at[t]))

    def product(j, q):
        units = pg_all[pl.ds(j * nr, nr)]
        weight = up[q * dq : (q + 1) * dq, :]
        if ts % 16 == 0:
            return lax.dot_general(units.reshape(tb, hc), weight, LAST, preferred_element_type=F32)
        return jnp.concatenate(
            [lax.dot_general(units[s], weight, LAST, preferred_element_type=F32) for s in range(nr)], axis=0)

    def sum_copy(j, q):
        return remote(gi_out.at[j, q], gi_in.at[jnp.where(c + 1 == j, j, jnp.where(c - 1 == j, nc, j)), q],
                      gi_s.at[j, q], gi_r.at[jnp.where(c + 1 == j, j, jnp.where(c - 1 == j, nc, j)), q],
                      {"col": jnp.where(j > c, c + 1, c - 1)})

    def sum_arrival(slot, q):
        remote(gi_out.at[0, q], gi_in.at[slot, q], gi_s.at[0, q], gi_r.at[slot, q],
               {"col": jnp.where(c > 0, c - 1, c + 1)}).wait_recv()

    def sum_first(j, q):
        gi_out[j, q] = product(j, q).astype(BF16)
        sum_copy(j, q).start()

    def sum_onward(j, q):
        gi_acc[...] = product(j, q)
        sum_arrival(j, q)
        gi_out[j, q] = (gi_acc[...] + gi_in[j, q].astype(F32)).astype(BF16)
        sum_copy(j, q).start()

    def own_product():
        for q in range(nq):
            gi_own[q] = product(c, q)

    def own_sum(q):
        @pl.when(c > 0)
        def _():
            sum_arrival(c, q)
            gi_own[q] += gi_in[c, q].astype(F32)

        @pl.when(c < nc - 1)
        def _():
            sum_arrival(nc, q)
            gi_own[q] += gi_in[nc, q].astype(F32)

        gi_ref[:, q * dq : (q + 1) * dq] = gi_own[q].astype(BF16)

    def gd_copy(i):
        slot = i % 2
        return pltpu.make_async_copy(gd_buf.at[slot], gd_out.at[pl.ds(i * gb, gb)], gd_o.at[slot])

    def gd_tile(i):
        @pl.when(i >= 2)
        def _():
            gd_copy(i - 2).wait()

        tile = act_all[:, :, pl.ds(pl.multiple_of(i * gb, gb), gb)]
        if ts % 16 == 0:
            tile = tile.reshape(tb * nc, gb)
        else:
            tile = tile.astype(F32).reshape(tb * nc, gb).astype(BF16)
        gd_buf[i % 2] = lax.dot_general(
            tile, cot_all[...].reshape(tb * nc, dr), FIRST, preferred_element_type=F32) * token_scale
        gd_copy(i).start()

    def x_on(step):
        for direction, far in ((0, c), (1, nc - 1 - c)):
            t = step - far
            j = c - t if direction == 0 else c + t
            jj = jnp.clip(j, 0, nc - 1)
            fits = (t >= 0) & (t <= far) & (far < nc - 1)

            @pl.when(fits & (t > 0))
            def _():
                line(x_all, x_s, x_r, direction, jj, x_all.at[jj]).wait_recv()

            @pl.when(fits)
            def _():
                line(x_all, x_s, x_r, direction, jj, x_all.at[jj]).start()

    def x_put(j):
        return pltpu.make_async_copy(x_all.at[j], x_out.at[j], x_o.at[j])

    def x_rest():
        x_put(c).start()
        for direction, far in ((0, c), (1, nc - 1 - c)):
            for t in range(1, nc):
                j = c - t if direction == 0 else c + t
                jj = jnp.clip(j, 0, nc - 1)

                @pl.when((far == nc - 1))
                def _():
                    line(x_all, x_s, x_r, direction, jj, x_all.at[jj]).wait_recv()

                @pl.when((j >= 0) & (j < nc))
                def _():
                    x_put(jj).start()

    local[4].wait()
    for step in range(nc):
        if step == 1:
            local[3].wait()
        if step > 0:
            pass_on(cot_all, cot_s, cot_r, cot_ref, step)
        x_on(step)
        s0(step)
        if step == 0:
            local[2].wait()
            activate_row(r, False)
        s1(step)
        if step == 1:
            activate_row(mate_row, True)
        if step >= 1:
            s2(step - 1)
        if step >= 2:
            s3(step - 2)
    for t in range(nc - 2):
        pg_ready(t)
    own_product()
    s3(nc - 2)
    pg_ready(nc - 2)

    @pl.when(end)
    def _():
        def body(t, _):
            j = jnp.where(c == 0, t, nc - 1 - t)
            for q in range(nq):
                sum_first(j, q)
            return 0

        lax.fori_loop(1, nc - 1, body, 0)

    s2(nc - 1)
    pre_rest()
    for step in range(nc, 2 * nc - 3):
        x_on(step)
    s3(nc - 1)
    pg_ready(nc - 1)

    orders = visit_order(nc)
    tiles = hc // gb
    slots = 2 * nq
    share = -(-tiles // slots)

    def gd_some(slot):
        lo, hi = min(slot * share, tiles), min((slot + 1) * share, tiles)
        if hi - lo == 1:
            gd_tile(jnp.int32(lo))
        elif hi > lo:
            lax.fori_loop(lo, hi, lambda i, _: (gd_tile(i), 0)[1], 0)

    @pl.when(end)
    def _():
        j = jnp.where(c == 0, nc - 1, 0)
        for q in range(nq):
            sum_first(j, q)

    for n in range(nc - 2):
        @pl.when(jnp.logical_not(end))
        def _():
            j = pick([order[n] for order in orders], c)
            for q in range(nq):
                sum_onward(j, q)

    pre_spread()
    activate_rest()
    for q in range(nq):
        @pl.when(jnp.logical_not(end))
        def _():
            sum_onward(pick([order[nc - 2] for order in orders], c), q)

        gd_some(q)
    x_rest()
    for q in range(nq):
        own_sum(q)
        gd_some(nq + q)

    for copy in ends:
        copy.wait_send()
    for i in range(nc):
        for n in range(nx):
            pre_send(i, n)[0].wait_send()
    def relay_end(unit, _):
        pl.when(pre_unit(unit)[1])(pre_relay(unit).wait_send)
        return 0

    lax.fori_loop(0, nc * nr, relay_end, 0)

    def sum_end(j, _):
        @pl.when(j != c)
        def _():
            for q in range(nq):
                sum_copy(j, q).wait_send()
        return 0

    lax.fori_loop(0, nc, sum_end, 0)
    finish_line(cot_all, cot_s, cot_r)
    finish_line(x_all, x_s, x_r)
    for copy in outs:
        copy.wait()
    for j in range(nc):
        x_put(j).wait()
    for i in range(max(0, tiles - 2), tiles):
        gd_copy(i).wait()


def tail(x_ref, pg_ref, gd_in, gi_in, gu_ref, gd_ref, gi_ref):
    token_scale = 1.0 / math.sqrt(pg_ref.shape[0])
    gu_ref[...] = lax.dot_general(x_ref[...], pg_ref[...], FIRST, preferred_element_type=F32) * token_scale
    gd_ref[...] = gd_in[...]

    @pl.when(pl.program_id(0) == 0)
    def _():
        gi_ref[...] = gi_in[...]


def per_device(nr, nc, inputs, cotangent, preactivation, up_weight, down_weight):
    tb, dr = inputs.shape
    hc = up_weight.shape[1]
    ts, nx = tb // nr, nr // 2
    tokens = tb * nc
    dq, gb = min(256, dr), min(256, hc)
    nq = dr // dq
    dma = pltpu.SemaphoreType.DMA
    anywhere = pl.BlockSpec(memory_space=pl.ANY)
    shape = jax.ShapeDtypeStruct
    gi, x_all, pg_all, gd = pl.pallas_call(
        functools.partial(kernel, nr, nc),
        out_shape=(
            shape((tb, dr), BF16), shape((nc, tb, dr), BF16),
            shape((nc * nr, ts, hc), BF16), shape((hc, dr), F32),
        ),
        in_specs=[anywhere] * 5,
        out_specs=(pl.BlockSpec(memory_space=pltpu.VMEM),) + (anywhere,) * 3,
        scratch_shapes=[
            pltpu.VMEM((nc, tb, dr), BF16), pltpu.VMEM((nc, tb, dr), BF16),
            pltpu.VMEM((nc * nr, ts, hc), BF16), pltpu.VMEM((nc * nr, ts, hc), BF16),
            pltpu.VMEM((nc * nr, ts, hc), BF16),
            pltpu.VMEM(up_weight.shape, BF16), pltpu.VMEM(down_weight.shape, BF16),
            pltpu.VMEM((nc, nr, ts, hc), F32),
            pltpu.VMEM((nc, nx, ts, hc), BF16), pltpu.VMEM((nc, nx, ts, hc), BF16),
            pltpu.VMEM((nc, nx - 1, ts, hc), BF16), pltpu.VMEM((nc, nx - 1, ts, hc), BF16),
            pltpu.VMEM((nq, tb, dq), F32), pltpu.VMEM((tb, dq), F32),
            pltpu.VMEM((nc, nq, tb, dq), BF16), pltpu.VMEM((nc + 1, nq, tb, dq), BF16),
            pltpu.VMEM((2, gb, dr), F32),
            dma((5,)), dma((2, nc)), dma((nc,)), dma((2, nc)), dma((nc,)),
            dma((nc, nx)), dma((nc * nr,)), dma((nc * nr,)), dma((nc,)), dma((nc,)),
            dma((nc, nx - 1)), dma((nc, nx - 1)), dma((nc, 2 * nx)), dma((nc, nr)),
            dma((nc, nq)), dma((nc + 1, nq)),
            dma((nc,)), dma((nc,)), dma((2,)),
        ],
        compiler_params=pltpu.CompilerParams(
            collective_id=0, has_side_effects=True, vmem_limit_bytes=60 * 1024 * 1024
        ),
    )(inputs, cotangent, preactivation.reshape(nc, ts, hc), up_weight, down_weight)
    steps = dr // dq
    gb = hc // steps
    grad_up, grad_down, grad_input = pl.pallas_call(
        tail,
        grid=(steps,),
        out_shape=(shape((dr, hc), F32), shape((hc, dr), F32), shape((tb, dr), BF16)),
        in_specs=[
            pl.BlockSpec((tokens, dq), lambda i: (0, i)),
            pl.BlockSpec((tokens, hc), lambda i: (0, 0), pipeline_mode=pl.Buffered(1)),
            pl.BlockSpec((gb, dr), lambda i: (i, 0)),
            pl.BlockSpec((tb, dr), lambda i: (0, 0), pipeline_mode=pl.Buffered(1)),
        ],
        out_specs=(
            pl.BlockSpec((dq, hc), lambda i: (i, 0)),
            pl.BlockSpec((gb, dr), lambda i: (i, 0)),
            pl.BlockSpec((tb, dr), lambda i: (0, 0)),
        ),
        compiler_params=pltpu.CompilerParams(vmem_limit_bytes=48 * 1024 * 1024),
    )(x_all.reshape(tokens, dr), pg_all.reshape(tokens, hc), gd, gi)
    return (grad_input, grad_up, grad_down)


def solution(mesh):
    placed = (
        P(("groups", "col"), "row"),
        P(("groups", "col"), "row"),
        P(("groups", "row"), "col"),
        P("row", "col"),
        P("col", "row"),
    )
    return jax.shard_map(
        functools.partial(per_device, mesh.shape["row"], mesh.shape["col"]),
        mesh=mesh,
        in_specs=placed,
        out_specs=(
            P(("groups", "col"), "row"),
            P(("groups", "row"), "col"),
            P(("groups", "col"), "row"),
        ),
        check_vma=False,
    )
```

```python
import functools
import math

import jax
import jax.numpy as jnp
from jax import lax
from jax.experimental import pallas as pl
from jax.experimental.pallas import tpu as pltpu
from jax.sharding import PartitionSpec as P

F32, BF16 = jnp.float32, jnp.bfloat16
LAST = (((1,), (1,)), ((), ()))
FIRST = (((0,), (0,)), ((), ()))


def tanh_of(v):
    return jnp.tanh(0.7978845608 * (v + 0.044715 * v * v * v))


def gelu_value(values):
    v = values.astype(F32)
    return 0.5 * v * (1.0 + tanh_of(v))


def gelu_pair(values):
    v = values.astype(F32)
    t = tanh_of(v)
    slope = 0.5 * (1.0 + t) + 0.5 * v * (1.0 - t * t) * 0.7978845608 * (1.0 + 3.0 * 0.044715 * v * v)
    return 0.5 * v * (1.0 + t), slope


def remote(src, dst, send, recv, where):
    return pltpu.make_async_remote_copy(
        src_ref=src, dst_ref=dst, send_sem=send, recv_sem=recv, device_id=where,
        device_id_type=pl.DeviceIdType.MESH,
    )


def pick(table, c):
    value = table[0]
    for at, other in enumerate(table):
        if at > 0:
            value = jnp.where(c == at, other, value)
    return value


def sum_plan(nc, nq):
    orders, events = [], []
    for c in range(nc):
        ranked = sorted((j, c, j) if j > c else (nc - 1 - j, nc - 1 - c, j) for j in range(nc) if j != c)
        orders.append([j for _, _, j in ranked])
        pieces = [(key, 2.2 * hops + q, n, q) for n, (key, hops, _) in enumerate(ranked) if n > 0 for q in range(nq)]
        events.append([(n, q) for _, _, n, q in sorted(pieces)])
    return orders, events


def block_at(c, t, nc):
    near = jnp.minimum(c, nc - 1 - c)
    step = -((t + 1) // 2) if t % 2 else t // 2
    return jnp.where(t <= 2 * near, c + step, jnp.where(2 * c < nc - 1, t, nc - 1 - t))


def kernel(
    nr, nc,
    x_ref, cot_ref, pre_ref, up_ref, down_ref,
    *rest,
):
    gi_ref, x_out, pg_out, gd_out = rest[:4]
    (
    x_all, cot_all, pre_all, act_all, pg_all, up, down, part, h1_out, h1_in, h2_out, h2_in,
    gi_own, gi_acc, gi_part, gi_out, gi_in, gd_buf,
    loc, cot_s, cot_r, x_s, x_r, pre_s, pre_on, pre_r, h1_s, h1_r, h2_s, h2_r, pg_s, pg_r, gi_s, gi_r,
    x_o, pg_o, gd_o, gi_o,
    ) = rest[4:]
    r, c = lax.axis_index("row"), lax.axis_index("col")
    nx = nr // 2
    x, k = r // 2, r % 2
    mate_row = 2 * x + (1 - k)
    mate = {"row": mate_row}
    tb, dr = x_ref.shape
    ts, hc = pg_all.shape[1:]
    nq, dq = gi_out.shape[1], gi_out.shape[3]
    hb, eb, gb = min(512, hc), min(256, hc), gd_buf.shape[1]
    peers = [(x + d) % nx for d in range(1, nx)]
    token_scale = 1.0 / math.sqrt(tb * nc)
    end = (c == 0) | (c == nc - 1)
    ends = []

    barrier = pltpu.get_barrier_semaphore()
    for d in range(1, nr):
        pl.semaphore_signal(barrier, inc=1, device_id={"row": (r + d) % nr}, device_id_type=pl.DeviceIdType.MESH)
    for d in range(1, nc):
        pl.semaphore_signal(barrier, inc=1, device_id={"col": (c + d) % nc}, device_id_type=pl.DeviceIdType.MESH)
    local = [
        pltpu.make_async_copy(cot_ref, cot_all.at[c], loc.at[0]),
        pltpu.make_async_copy(down_ref, down, loc.at[1]),
        pltpu.make_async_copy(pre_ref, pre_all.at[pl.ds(r * nc, nc)], loc.at[2]),
        pltpu.make_async_copy(up_ref, up, loc.at[3]),
        pltpu.make_async_copy(x_ref, x_all.at[c], loc.at[4]),
    ]
    for copy in local[:3]:
        copy.start()
    pl.semaphore_wait(barrier, nr + nc - 2)

    def started(copy):
        copy.start()
        ends.append(copy)

    def line(all_ref, send, recv, direction, j, source):
        return remote(source, all_ref.at[j], send.at[direction, j], recv.at[j],
                      {"col": c + 1 if direction == 0 else c - 1})

    def pass_on(all_ref, send, recv, own_ref, t):
        for direction, j in ((0, c - t), (1, c + t)):
            there = (j >= 0) & (j < nc)
            onward = (c + 1 < nc) if direction == 0 else (c >= 1)
            jj = jnp.clip(j, 0, nc - 1)
            if t > 0:
                @pl.when(there)
                def _():
                    line(all_ref, send, recv, direction, jj, all_ref.at[jj]).wait_recv()

            @pl.when(there & onward)
            def _():
                src = own_ref if t == 0 else all_ref.at[jj]
                line(all_ref, send, recv, direction, jj, src).start()

    def finish_line(all_ref, send, recv):
        for t in range(nc):
            for direction, j in ((0, c - t), (1, c + t)):
                onward = (c + 1 < nc) if direction == 0 else (c >= 1)
                jj = jnp.clip(j, 0, nc - 1)

                @pl.when((j >= 0) & (j < nc) & onward)
                def _():
                    line(all_ref, send, recv, direction, jj, all_ref.at[jj]).wait_send()

    def pre_send(i, n):
        unit = r * nc + i
        user = unit % nr
        if n == nx - 1:
            target, first = mate_row, True
        else:
            first = user // 2 == peers[n]
            target = jnp.where(first, user, 2 * peers[n] + k)
        return remote(pre_ref.at[i], pre_all.at[unit], pre_s.at[i, n], pre_r.at[unit], {"row": target}), first

    def pre_unit(unit):
        source, user = unit // nc, unit % nr
        away = source // 2 != x
        straight = jnp.where(user // 2 == x, user == r, source % 2 == k)
        return away, away & straight, user == r

    def pre_relay(unit):
        return remote(pre_all.at[unit], pre_all.at[unit], pre_on.at[unit], pre_r.at[unit], mate)

    def pre_arrival(unit):
        pre_relay(unit).wait_recv()

    pass_on(cot_all, cot_s, cot_r, cot_ref, 0)
    for early in (True, False):
        for i in range(nc):
            for n in range(nx - 1) if early else (nx - 1,):
                copy, first = pre_send(i, n)
                if early:
                    pl.when(first)(copy.start)
                else:
                    copy.start()

    def pre_rest():
        for i in range(nc):
            for n in range(nx - 1):
                copy, first = pre_send(i, n)
                pl.when(jnp.logical_not(first))(copy.start)

    def pre_spread():
        def body(unit, _):
            away, straight, mine = pre_unit(unit)

            @pl.when(straight & jnp.logical_not(mine))
            def _():
                pre_arrival(unit)

            @pl.when(straight)
            def _():
                pre_relay(unit).start()
            return 0

        lax.fori_loop(0, nc * nr, body, 0)

    def activate_unit(unit):
        def body(i, _):
            at = pl.ds(pl.multiple_of(i * eb, eb), eb)
            act_all[unit, :, at] = gelu_value(pre_all[unit, :, at]).astype(BF16)
            return 0

        lax.fori_loop(0, hc // eb, body, 0)

    def activate_row(row, wait):
        def body(i, _):
            unit = row * nc + i
            if wait:
                pre_arrival(unit)
            activate_unit(unit)
            return 0

        lax.fori_loop(0, nc, body, 0)

    def activate_rest():
        def body(unit, _):
            away, straight, mine = pre_unit(unit)

            @pl.when(away & jnp.logical_not(straight))
            def _():
                pre_arrival(unit)

            @pl.when(away & jnp.logical_not(mine))
            def _():
                activate_unit(unit)
            return 0

        lax.fori_loop(0, nc * nr, body, 0)

    def s0(t):
        j = block_at(c, t, nc)
        if t == 0:
            local[0].wait()
            local[1].wait()
        block = cot_all[j]

        def body(i, _):
            at = pl.ds(pl.multiple_of(i * hb, hb), hb)
            got = lax.dot_general(block, down[at, :], LAST, preferred_element_type=F32)
            for s in range(nr):
                part[t, s, :, at] = got[s * ts : (s + 1) * ts]
            return 0

        lax.fori_loop(0, hc // hb, body, 0)
        for p in range(nx):
            h1_out[t, p] = part[t, 2 * p + (1 - k)].astype(BF16)
        started(remote(h1_out.at[t], h1_in.at[t], h1_s.at[t], h1_r.at[t], mate))

    def s1(t):
        remote(h1_out.at[t], h1_in.at[t], h1_s.at[t], h1_r.at[t], mate).wait_recv()
        for i, p in enumerate(peers):
            h2_out[t, i] = (part[t, 2 * p + k] + h1_in[t, p].astype(F32)).astype(BF16)
            started(remote(h2_out.at[t, i], h2_in.at[t, i], h2_s.at[t, i], h2_r.at[t, i],
                           {"row": 2 * p + k}))

    def pg_copy(t, index, source_row, target_row):
        unit = pg_all.at[block_at(c, t, nc) * nr + source_row]
        return remote(unit, unit, pg_s.at[t, index], pg_r.at[t, source_row], {"row": target_row})

    def s2(t):
        for i, p in enumerate(peers):
            remote(h2_out.at[t, i], h2_in.at[t, i], h2_s.at[t, i], h2_r.at[t, i],
                   {"row": 2 * p + k}).wait_recv()
        j = block_at(c, t, nc)
        unit = j * nr + r

        @pl.when((unit // nc) // 2 != x)
        def _():
            pre_arrival(unit)

        def body(i, _):
            at = pl.ds(pl.multiple_of(i * eb, eb), eb)
            total = part[t, 2 * x + k, :, at] + h1_in[t, x, :, at].astype(F32)
            for i in range(nx - 1):
                total += h2_in[t, i, :, at].astype(F32)
            value, slope = gelu_pair(pre_all[unit, :, at])
            act_all[unit, :, at] = value.astype(BF16)
            pg_all[unit, :, at] = (total * slope).astype(BF16)
            return 0

        lax.fori_loop(0, hc // eb, body, 0)
        for i, p in enumerate(peers):
            started(pg_copy(t, 1 + i, r, 2 * p + k))
        started(pg_copy(t, 0, r, mate_row))

    def s3(t):
        for i, p in enumerate(peers):
            pg_copy(t, 0, 2 * p + k, mate_row).wait_recv()
            started(pg_copy(t, nx + i, 2 * p + k, mate_row))

    outs = []

    def put_out(copy):
        copy.start()
        outs.append(copy)

    def pg_ready(t):
        for p in range(nx):
            pg_copy(t, 0, 2 * p + (1 - k), mate_row).wait_recv()
        units = pl.ds(block_at(c, t, nc) * nr, nr)
        put_out(pltpu.make_async_copy(pg_all.at[units], pg_out.at[units], pg_o.at[t]))

    def product(j, q):
        units = pg_all[pl.ds(j * nr, nr)]
        weight = up[q * dq : (q + 1) * dq, :]
        if ts % 16 == 0:
            return lax.dot_general(units.reshape(tb, hc), weight, LAST, preferred_element_type=F32)
        return jnp.concatenate(
            [lax.dot_general(units[s], weight, LAST, preferred_element_type=F32) for s in range(nr)], axis=0)

    def sum_copy(j, q):
        return remote(gi_out.at[j, q], gi_in.at[jnp.where(c + 1 == j, j, jnp.where(c - 1 == j, nc, j)), q],
                      gi_s.at[j, q], gi_r.at[jnp.where(c + 1 == j, j, jnp.where(c - 1 == j, nc, j)), q],
                      {"col": jnp.where(j > c, c + 1, c - 1)})

    def sum_arrival(slot, q):
        remote(gi_out.at[0, q], gi_in.at[slot, q], gi_s.at[0, q], gi_r.at[slot, q],
               {"col": jnp.where(c > 0, c - 1, c + 1)}).wait_recv()

    def sum_first(j, q):
        gi_acc[...] = product(j, q)
        gi_out[j, q] = gi_acc[...].astype(BF16)
        sum_copy(j, q).start()

    def sum_onward(j, q):
        gi_acc[...] = product(j, q)
        sum_arrival(j, q)
        gi_out[j, q] = (gi_acc[...] + gi_in[j, q].astype(F32)).astype(BF16)
        sum_copy(j, q).start()

    def own_product():
        for q in range(nq):
            gi_own[q] = product(c, q)

    def own_sum(q):
        @pl.when(c > 0)
        def _():
            sum_arrival(c, q)
            gi_own[q] += gi_in[c, q].astype(F32)

        @pl.when(c < nc - 1)
        def _():
            sum_arrival(nc, q)
            gi_own[q] += gi_in[nc, q].astype(F32)

        gi_out[c, q] = gi_own[q].astype(BF16)
        put_out(pltpu.make_async_copy(gi_out.at[c, q], gi_ref.at[q], gi_o.at[q]))

    def gd_copy(i):
        slot = i % 2
        return pltpu.make_async_copy(gd_buf.at[slot], gd_out.at[pl.ds(i * gb, gb)], gd_o.at[slot])

    def gd_tile(i):
        @pl.when(i >= 2)
        def _():
            gd_copy(i - 2).wait()

        tile = act_all[:, :, pl.ds(pl.multiple_of(i * gb, gb), gb)]
        if ts % 16 == 0:
            tile = tile.reshape(tb * nc, gb)
        else:
            tile = tile.astype(F32).reshape(tb * nc, gb).astype(BF16)
        gd_buf[i % 2] = lax.dot_general(
            tile, cot_all[...].reshape(tb * nc, dr), FIRST, preferred_element_type=F32) * token_scale
        gd_copy(i).start()

    def x_on(step):
        for direction, far in ((0, c), (1, nc - 1 - c)):
            t = step - far
            j = c - t if direction == 0 else c + t
            jj = jnp.clip(j, 0, nc - 1)
            fits = (t >= 0) & (t <= far) & (far < nc - 1)

            @pl.when(fits & (t > 0))
            def _():
                line(x_all, x_s, x_r, direction, jj, x_all.at[jj]).wait_recv()

            @pl.when(fits)
            def _():
                line(x_all, x_s, x_r, direction, jj, x_all.at[jj]).start()

    def x_put(j):
        return pltpu.make_async_copy(x_all.at[j], x_out.at[j], x_o.at[j])

    def x_rest():
        x_put(c).start()
        for direction, far in ((0, c), (1, nc - 1 - c)):
            for t in range(1, nc):
                j = c - t if direction == 0 else c + t
                jj = jnp.clip(j, 0, nc - 1)

                @pl.when((far == nc - 1))
                def _():
                    line(x_all, x_s, x_r, direction, jj, x_all.at[jj]).wait_recv()

                @pl.when((j >= 0) & (j < nc))
                def _():
                    x_put(jj).start()

    def sum_near(t):
        @pl.when(end)
        def _():
            for q in range(nq):
                sum_first(jnp.where(c == 0, t, nc - 1 - t), q)

    last = nc - 1
    for step in range(nc):
        if step > 0:
            pass_on(cot_all, cot_s, cot_r, cot_ref, step)
            x_on(step - 1)
        s0(step)
        if step == 0:
            local[3].start()
            local[4].start()
            local[2].wait()
            activate_row(r, False)
        s1(step)
        if step == 0:
            local[3].wait()
            local[4].wait()
        if step == 1:
            activate_row(mate_row, True)
        if step >= 2:
            s3(step - 1)
            pg_ready(step - 1)
            sum_near(step - 1)
        if 1 <= step < last:
            s2(step)
    x_on(last)
    s2(last)
    s2(0)
    pre_rest()
    for step in range(nc, 2 * nc - 3):
        x_on(step)
    orders, events = sum_plan(nc, nq)

    def pass_first():
        @pl.when(jnp.logical_not(end))
        def _():
            j = pick([order[0] for order in orders], c)
            for q in range(nq):
                sum_onward(j, q)

    def pass_later(lo, hi):
        for e in range(lo, hi):
            @pl.when(jnp.logical_not(end))
            def _():
                n, q = (pick([plan[e][at] for plan in events], c) for at in (0, 1))
                j = pick([order[plan[e][0]] for order, plan in zip(orders, events)], c)
                sum_arrival(j, q)
                gi_out[j, q] = (gi_part[n - 1, q] + gi_in[j, q].astype(F32)).astype(BF16)
                sum_copy(j, q).start()

    if nc > 3:
        pass_first()
    s3(last)
    pg_ready(last)
    sum_near(last)
    if nc == 3:
        pass_first()

    @pl.when(jnp.logical_not(end))
    def _():
        for n in range(1, nc - 1):
            j = pick([order[n] for order in orders], c)
            for q in range(nq):
                gi_part[n - 1, q] = product(j, q)

    count = len(events[0])
    pass_later(0, count // 4)
    s3(0)
    pg_ready(0)
    own_product()
    pass_later(count // 4, 3 * count // 4)
    pre_spread()
    activate_rest()
    x_rest()
    pass_later(3 * count // 4, count)
    tiles = hc // gb
    share = -(-tiles // nq)
    for q in range(nq):
        lo, hi = min(q * share, tiles), min((q + 1) * share, tiles)
        if hi > lo:
            lax.fori_loop(lo, hi, lambda i, _: (gd_tile(i), 0)[1], 0)
        own_sum(q)

    for copy in ends:
        copy.wait_send()
    for i in range(nc):
        for n in range(nx):
            pre_send(i, n)[0].wait_send()
    def relay_end(unit, _):
        pl.when(pre_unit(unit)[1])(pre_relay(unit).wait_send)
        return 0

    lax.fori_loop(0, nc * nr, relay_end, 0)

    def sum_end(j, _):
        @pl.when(j != c)
        def _():
            for q in range(nq):
                sum_copy(j, q).wait_send()
        return 0

    lax.fori_loop(0, nc, sum_end, 0)
    finish_line(cot_all, cot_s, cot_r)
    finish_line(x_all, x_s, x_r)
    for copy in outs:
        copy.wait()
    for j in range(nc):
        x_put(j).wait()
    for i in range(max(0, tiles - 2), tiles):
        gd_copy(i).wait()


def tail(x_ref, pg_ref, gd_in, gi_in, gu_ref, gd_ref, gi_ref, x, pg, gu, gd, gi, loads, gd_loads, stores):
    token_scale = 1.0 / math.sqrt(pg_ref.shape[0])
    parts, tokens, cols = pg.shape
    blocks, rows = gd.shape[:2]
    nq, dq = gi_in.shape[0], gi_in.shape[2]
    read = pltpu.make_async_copy
    x_load = read(x_ref, x, loads.at[parts])
    pg_load = [read(pg_ref.at[:, pl.ds(n * cols, cols)], pg.at[n], loads.at[n]) for n in range(parts)]
    gi_load = read(gi_in, gi, loads.at[parts + 1])
    gd_load = [read(gd_in.at[pl.ds(n * rows, rows)], gd.at[n], gd_loads.at[n]) for n in range(blocks)]
    gu_store = [read(gu.at[n], gu_ref.at[:, pl.ds(n * cols, cols)], stores.at[n]) for n in range(parts)]
    gi_store = [read(gi.at[q], gi_ref.at[:, pl.ds(q * dq, dq)], loads.at[q]) for q in range(nq)]
    gd_store = [read(gd.at[n], gd_ref.at[pl.ds(n * rows, rows)], gd_loads.at[n]) for n in range(blocks)]
    x_load.start()
    for copy in pg_load + gd_load + [gi_load]:
        copy.start()
    x_load.wait()
    each = -(-blocks // parts)
    for n in range(parts):
        pg_load[n].wait()
        gu[n] = lax.dot_general(x[...], pg[n], FIRST, preferred_element_type=F32) * token_scale
        gu_store[n].start()
        for m in range(n * each, min((n + 1) * each, blocks)):
            gd_load[m].wait()
            gd_store[m].start()
    gi_load.wait()
    for copy in gi_store:
        copy.start()
    for copy in gu_store + gd_store + gi_store:
        copy.wait()


def per_device(nr, nc, inputs, cotangent, preactivation, up_weight, down_weight):
    tb, dr = inputs.shape
    hc = up_weight.shape[1]
    ts, nx = tb // nr, nr // 2
    tokens = tb * nc
    dq, gb = min(256, dr), min(256, hc)
    nq = dr // dq
    dma = pltpu.SemaphoreType.DMA
    anywhere = pl.BlockSpec(memory_space=pl.ANY)
    shape = jax.ShapeDtypeStruct
    scratch = [
        pltpu.VMEM((nc, tb, dr), BF16), pltpu.VMEM((nc, tb, dr), BF16),
        pltpu.VMEM((nc * nr, ts, hc), BF16), pltpu.VMEM((nc * nr, ts, hc), BF16),
        pltpu.VMEM((nc * nr, ts, hc), BF16),
        pltpu.VMEM(up_weight.shape, BF16), pltpu.VMEM(down_weight.shape, BF16),
        pltpu.VMEM((nc, nr, ts, hc), F32),
        pltpu.VMEM((nc, nx, ts, hc), BF16), pltpu.VMEM((nc, nx, ts, hc), BF16),
        pltpu.VMEM((nc, nx - 1, ts, hc), BF16), pltpu.VMEM((nc, nx - 1, ts, hc), BF16),
        pltpu.VMEM((nq, tb, dq), F32), pltpu.VMEM((tb, dq), F32), pltpu.VMEM((nc - 2, nq, tb, dq), F32),
        pltpu.VMEM((nc, nq, tb, dq), BF16), pltpu.VMEM((nc + 1, nq, tb, dq), BF16),
        pltpu.VMEM((2, gb, dr), F32),
        dma((5,)), dma((2, nc)), dma((nc,)), dma((2, nc)), dma((nc,)),
        dma((nc, nx)), dma((nc * nr,)), dma((nc * nr,)), dma((nc,)), dma((nc,)),
        dma((nc, nx - 1)), dma((nc, nx - 1)), dma((nc, 2 * nx)), dma((nc, nr)),
        dma((nc, nq)), dma((nc + 1, nq)),
        dma((nc,)), dma((nc,)), dma((2,)), dma((nq,)),
    ]
    gi, x_all, pg_all, gd = pl.pallas_call(
        functools.partial(kernel, nr, nc),
        out_shape=(
            shape((nq, tb, dq), BF16), shape((nc, tb, dr), BF16),
            shape((nc * nr, ts, hc), BF16), shape((hc, dr), F32),
        ),
        in_specs=[anywhere] * 5,
        out_specs=(anywhere,) * 4,
        scratch_shapes=scratch,
        compiler_params=pltpu.CompilerParams(
            collective_id=0, has_side_effects=True, vmem_limit_bytes=60 * 1024 * 1024
        ),
    )(inputs, cotangent, preactivation.reshape(nc, ts, hc), up_weight, down_weight)
    cols, rows = min(512, hc), min(256, hc)
    parts, blocks = hc // cols, hc // rows
    grad_up, grad_down, grad_input = pl.pallas_call(
        tail,
        out_shape=(shape((dr, hc), F32), shape((hc, dr), F32), shape((tb, dr), BF16)),
        in_specs=[anywhere] * 4,
        out_specs=(anywhere,) * 3,
        scratch_shapes=[
            pltpu.VMEM((tokens, dr), BF16), pltpu.VMEM((parts, tokens, cols), BF16),
            pltpu.VMEM((parts, dr, cols), F32), pltpu.VMEM((blocks, rows, dr), F32),
            pltpu.VMEM((nq, tb, dq), BF16),
            dma((max(parts + 2, nq),)), dma((blocks,)), dma((parts,)),
        ],
        compiler_params=pltpu.CompilerParams(vmem_limit_bytes=60 * 1024 * 1024),
    )(x_all.reshape(tokens, dr), pg_all.reshape(tokens, hc), gd, gi)
    return (grad_input, grad_up, grad_down)


def solution(mesh):
    placed = (
        P(("groups", "col"), "row"),
        P(("groups", "col"), "row"),
        P(("groups", "row"), "col"),
        P("row", "col"),
        P("col", "row"),
    )
    return jax.shard_map(
        functools.partial(per_device, mesh.shape["row"], mesh.shape["col"]),
        mesh=mesh,
        in_specs=placed,
        out_specs=(
            P(("groups", "col"), "row"),
            P(("groups", "row"), "col"),
            P(("groups", "col"), "row"),
        ),
        check_vma=False,
    )
```
